128 devices in a mesh: req: 64 (over z, y, x), tp: 2 (over core).
Axes of the slice: x: 4, y: 4, z: 4, core: 2. Of those that a mesh axis runs over, the one named last changes fastest.
Arguments:
- tokens: bfloat16 [16384, 4096], P('req'), may hold values from -12 to 12, as said below
- layer_norm_gain: bfloat16 [4096], replicated, may hold values from 0.5 to 1.5
- query_key_value_weight: bfloat16 [4096, 3, 4096], P(None, None, 'tp'), may hold values from -1.5625 to 1.5625, as said below
- output_weight: bfloat16 [4096, 4096], P('tp'), may hold values from -0.09375 to 0.09375
- stored_down_weight: bfloat16 [256, 4096, 16], P('req', 'tp'), may hold values from -0.09375 to 0.09375
- stored_up_weight: bfloat16 [256, 16, 3, 4096], P('req', None, None, 'tp'), may hold values from -1.5 to 1.5
- group_prompt_length: int32 [64, 8], P('req'), may hold values from 1 to 64, as said below
- prompt_adapter_index: int32 [64, 8], P('req'), may hold values from 0 to 255, as said below
- placement: int32 [256], replicated, may hold values from 0 to 255, as said below
Outputs:
- block_out: bfloat16 [16384, 4096], P(('req', 'tp'))
The draws below stay inside these ranges and needn't reach their ends.
Inputs may be any that keep to these rules, and one draw needn't show every extreme that they name: `group_prompt_length`: each row sums to 256, and its largest entry is exactly 64. `prompt_adapter_index`: the prompts of one group use adapters whose storage rows lie on distinct indices of req (row placement[a] lies on index placement[a] // 4); the longest prompt of every group uses an adapter stored on one common index of req. `placement`: A permutation of the adapters. `tokens`: real values. `query_key_value_weight`: real values.
All inputs are finite; a program needn't handle non-finite values.
Results may differ from the reference program's by a relative error of at most 0.012.
Values may be sent and summed in bfloat16 or wider, within the bound.
No kernel may reach another device: no remote copies, remote signals or barrier semaphores. Data moves between devices by JAX's collectives and lax.ppermute only.
A program may use at most 448 MiB of HBM per device.

```python
import math
import jax
import jax.numpy as jnp
from jax import lax

HEADS = 32
HEAD_DIM = 128
MODEL_WIDTH = 4096
ADAPTER_RANK = 16
ADP_DEV = 4
ADAPTER_TOTAL = 256
TOK_DEV = 256
PROMPTS_PER_REQ = 8
MAXLEN = 64
TOKENS = 16384
N_REQ = 64
N_TP = 2


def routing_tables(key):
    base_projection = jax.random.fold_in(key, 7)
    place_key, hot_key, dev_key = jax.random.split(base_projection, 3)
    placement = jax.random.permutation(place_key, ADAPTER_TOTAL).astype(jnp.int32)
    holder = jnp.argsort(placement).astype(jnp.int32)
    hot = jax.random.randint(hot_key, (), 0, N_REQ)
    rest = TOK_DEV - MAXLEN
    spread = rest // (2 * (PROMPTS_PER_REQ - 1)) - 1
    marks = (jnp.arange(1, PROMPTS_PER_REQ - 1, dtype=jnp.int32) * rest // (PROMPTS_PER_REQ - 1)).astype(jnp.int32)

    def one_device(device_key):
        jitter_key, spot_key, peer_key, slot_key = jax.random.split(device_key, 4)
        cuts = marks + jax.random.randint(jitter_key, (PROMPTS_PER_REQ - 2,), -spread, spread + 1)
        edges = jnp.concatenate([jnp.zeros((1,), jnp.int32), cuts.astype(jnp.int32), jnp.full((1,), rest, jnp.int32)])
        parts = edges[1:] - edges[:-1]
        lengths = jnp.concatenate([jnp.full((1,), MAXLEN, jnp.int32), parts])
        peers = jax.random.permutation(peer_key, N_REQ - 1)[:PROMPTS_PER_REQ - 1] + 1
        offsets = jnp.concatenate([jnp.zeros((1,), jnp.int32), peers.astype(jnp.int32)])
        owners = (hot + offsets) % N_REQ
        local = jax.random.randint(slot_key, (PROMPTS_PER_REQ,), 0, ADP_DEV)
        adapters = holder[owners * ADP_DEV + local]
        spot = jax.random.randint(spot_key, (), 0, PROMPTS_PER_REQ)
        return (jnp.roll(lengths, spot), jnp.roll(adapters, spot))
    lengths, adapters = jax.vmap(one_device)(jax.random.split(dev_key, N_REQ))
    return (lengths.astype(jnp.int32), adapters.astype(jnp.int32), placement)


def draw_group_prompt_length(key, part):
    return routing_tables(key)[0]


def draw_prompt_adapter_index(key, part):
    return routing_tables(key)[1]


def draw_placement(key, part):
    return routing_tables(key)[2]


def draw_tokens(key, part):
    noise_key = jax.random.fold_in(jax.random.fold_in(key, 11), 0)
    values = jax.random.truncated_normal(noise_key, -5.0, 5.0, (TOKENS, MODEL_WIDTH), jnp.float32)
    return jnp.clip(values, -12.0, 12.0).astype(jnp.bfloat16)


def draw_query_key_value_weight(key, part):
    main_key = jax.random.fold_in(jax.random.fold_in(key, 13), 0)
    values = jax.random.truncated_normal(main_key, -4.0, 4.0, (MODEL_WIDTH, 3, MODEL_WIDTH), jnp.float32) / math.sqrt(MODEL_WIDTH)
    return values.astype(jnp.bfloat16)


def levels(key, dims, cuts, low, largest):
    level = 1.0
    for axis_at, blocks in cuts:
        heights = jax.random.uniform(jax.random.fold_in(jax.random.fold_in(key, 6), axis_at), (blocks,), jnp.float32, low / len(cuts), largest / len(cuts))
        level = level * jnp.repeat(jnp.exp(heights), dims[axis_at] // blocks).reshape((-1,) + (1,) * (len(dims) - 1 - axis_at))
    return level


def bell_draw(key, extent, deviation, most, pieces=(), kind=jnp.bfloat16):
    factor_of = levels(key, extent, pieces, -0.22, 0.18) if pieces else 1.0
    values = jax.random.normal(key, extent, jnp.float32) * deviation * factor_of
    return jnp.minimum(jnp.maximum(values, -most), most).astype(kind)


def setup_inputs(seed: int = 0) -> dict:
    streams_of = jax.random.split(jax.random.key(seed), 10)
    return {
        "tokens": draw_tokens(jax.random.fold_in(streams_of[9], 71), 0),
        "layer_norm_gain": jnp.clip(1.0 + 0.1 * jax.random.normal(streams_of[1], (MODEL_WIDTH,), jnp.float32), 0.5, 1.5).astype(jnp.bfloat16),
        "query_key_value_weight": draw_query_key_value_weight(jax.random.fold_in(streams_of[9], 71), 0),
        "output_weight": bell_draw(streams_of[3], (MODEL_WIDTH, MODEL_WIDTH), MODEL_WIDTH ** -0.5, 0.09375, ((0, 2),)),
        "stored_down_weight": bell_draw(streams_of[4], (ADAPTER_TOTAL, MODEL_WIDTH, ADAPTER_RANK), MODEL_WIDTH ** -0.5, 0.09375, ((0, 64), (1, 2))),
        "stored_up_weight": bell_draw(streams_of[5], (ADAPTER_TOTAL, ADAPTER_RANK, 3, MODEL_WIDTH), ADAPTER_RANK ** -0.5, 1.5, ((0, 64), (3, 2))),
        "group_prompt_length": draw_group_prompt_length(jax.random.fold_in(streams_of[9], 71), 0),
        "prompt_adapter_index": draw_prompt_adapter_index(jax.random.fold_in(streams_of[9], 71), 0),
        "placement": draw_placement(jax.random.fold_in(streams_of[9], 71), 0),
    }


LOWRANK_SCALE = 0.5
EPS = 1e-05

def reference(tokens, layer_norm_gain, query_key_value_weight, output_weight, stored_down_weight, stored_up_weight, group_prompt_length, prompt_adapter_index, placement):
    heads_f = jnp.arange(HEADS, dtype=jnp.float32)
    slopes = jnp.exp2(-8.0 * (heads_f + 1.0) / HEADS)
    scale = 1.0 / math.sqrt(HEAD_DIM)
    qkv_flat = query_key_value_weight.reshape(MODEL_WIDTH, 3 * MODEL_WIDTH)
    gain = layer_norm_gain.astype(jnp.float32)

    def one_group(group):
        rows, lengths, ids = group
        wide = rows.astype(jnp.float32)
        mean = lax.optimization_barrier(jnp.mean(wide, -1, keepdims=True))
        centred = wide - mean
        variance = lax.optimization_barrier(jnp.mean(centred * centred, -1, keepdims=True))
        normed = (centred * lax.rsqrt(variance + EPS) * gain).astype(jnp.bfloat16)
        ends = jnp.cumsum(lengths).astype(jnp.int32)
        index = jnp.arange(TOK_DEV, dtype=jnp.int32)
        segment = lax.optimization_barrier(jnp.sum((index[:, None] >= ends[None, :]).astype(jnp.int32), 1))
        table = jnp.arange(ADAPTER_TOTAL, dtype=jnp.int32)
        storage_slots = lax.optimization_barrier(jnp.sum(jnp.where(table[None, :] == ids[:, None], placement[None, :], 0), 1)).astype(jnp.int32)
        down_joined_rows = jnp.transpose(stored_down_weight[storage_slots], (1, 0, 2)).reshape(MODEL_WIDTH, PROMPTS_PER_REQ * ADAPTER_RANK)
        proj = jnp.dot(normed, down_joined_rows, preferred_element_type=jnp.float32)
        column_prompt = jnp.arange(PROMPTS_PER_REQ * ADAPTER_RANK, dtype=jnp.int32) // ADAPTER_RANK
        lowrank_activation = jnp.where(segment[:, None] == column_prompt[None, :], proj, 0.0).astype(jnp.bfloat16)
        up_joined_rows = stored_up_weight[storage_slots].reshape(PROMPTS_PER_REQ * ADAPTER_RANK, 3 * MODEL_WIDTH)
        lowrank_update = jnp.dot(lowrank_activation, up_joined_rows, preferred_element_type=jnp.float32).astype(jnp.bfloat16)
        base_projection = jnp.dot(normed, qkv_flat, preferred_element_type=jnp.float32)
        projected_rows = (base_projection + LOWRANK_SCALE * lowrank_update.astype(jnp.float32)).astype(jnp.bfloat16)
        projected_rows = projected_rows.reshape(TOK_DEV, 3, HEADS, HEAD_DIM)
        queries = projected_rows[:, 0].astype(jnp.float32)
        keys = projected_rows[:, 1].astype(jnp.float32)
        values = projected_rows[:, 2].astype(jnp.float32)
        scores = jnp.einsum('qhd,khd->hqk', queries, keys)
        allowed = (segment[:, None] == segment[None, :]) & (index[None, :] <= index[:, None])
        bias = slopes[:, None, None] * (index[None, None, :] - index[None, :, None]).astype(jnp.float32)
        scores = jnp.where(allowed[None], scores * scale + bias, -jnp.inf)
        top = lax.optimization_barrier(jnp.max(scores, -1, keepdims=True))
        weights = jnp.exp(scores - top)
        probs = (weights / lax.optimization_barrier(jnp.sum(weights, -1, keepdims=True))).astype(jnp.bfloat16)
        attended = jnp.einsum('hqk,khd->qhd', probs.astype(jnp.float32), values).astype(jnp.bfloat16)
        attended = attended.reshape(TOK_DEV, MODEL_WIDTH)
        share = MODEL_WIDTH // N_TP
        total = wide
        for block in range(N_TP):
            partial_value = jnp.dot(attended[:, block * share:(block + 1) * share], output_weight[block * share:(block + 1) * share], preferred_element_type=jnp.float32)
            total = total + lax.optimization_barrier(partial_value.astype(jnp.bfloat16)).astype(jnp.float32)
        return total.astype(jnp.bfloat16)
    grouped = tokens.reshape(N_REQ, TOK_DEV, MODEL_WIDTH)
    result = lax.map(one_group, (grouped, group_prompt_length, prompt_adapter_index))
    return result.reshape(TOKENS, MODEL_WIDTH)
```

```python
import math

import jax
import jax.numpy as jnp
from jax import lax
from jax.experimental import pallas as pl
from jax.experimental.pallas import tpu as pltpu
from jax.sharding import PartitionSpec as P

HEADS = 32
HEAD_DIM = 128
LOWRANK_SCALE = 0.5
EPS = 1e-05
RANK = 16
SIDE = 4
STRIDE = {"x": 1, "y": SIDE, "z": SIDE * SIDE}
SHIFT = {"x": 2, "y": 4, "z": 6}
AXES = (("z", "y", "x"), ("x", "z", "y"), ("y", "x", "z"))
INFO = 128


def ring(axis, step):
    stride = STRIDE[axis]
    pairs = []
    for r in range(SIDE**3):
        c = (r // stride) % SIDE
        pairs.append((r, r + ((c + step) % SIDE - c) * stride))
    return pairs


def shift(value, axis, step):
    return lax.ppermute(value, "req", ring(axis, step))


def field(slot, axis):
    return (slot >> SHIFT[axis]) & (SIDE - 1)


def start_item(slot, coords, axes, items, target, sem):
    a, b, _ = axes
    own, below, above, far0, far1 = items
    rel_a = (field(slot, a) - coords[a]) & 3
    rel_b = (field(slot, b) - coords[b]) & 3
    row = rel_a * 4 + (slot & 3)

    def from_(ref, at):
        return lambda: pltpu.make_async_copy(ref.at[at], target, sem).start()

    pl.when(rel_b == 0)(from_(own, row))
    pl.when(rel_b == 3)(from_(below, row))
    pl.when(rel_b == 1)(from_(above, row))
    pl.when((rel_b == 2) & (row < 8))(from_(far0, row & 7))
    pl.when((rel_b == 2) & (row >= 8))(from_(far1, row & 7))


def coords_of(ref):
    return {"x": ref[0], "y": ref[1], "z": ref[2]}


def any_spec():
    return pl.BlockSpec(memory_space=pl.ANY)


def vmem_spec():
    return pl.BlockSpec(memory_space=pltpu.VMEM)


def smem_spec():
    return pl.BlockSpec(memory_space=pltpu.SMEM)


def take_far(place, slots, items, axes, width):
    def kernel(place_ref, slot_ref, *refs):
        item_refs, (lo, hi), sems = refs[:5], refs[5:7], refs[7]
        coords = coords_of(place_ref)
        outs = [lo.at[i] for i in range(4)] + [hi.at[i] for i in range(4)]
        for i in range(8):
            start_item(slot_ref[i], coords, axes, item_refs, outs[i], sems.at[i])
        for i in range(8):
            pltpu.make_async_copy(item_refs[0].at[0], outs[i], sems.at[i]).wait()

    half = jax.ShapeDtypeStruct((4, RANK, width), jnp.bfloat16)
    return pl.pallas_call(
        kernel,
        out_shape=(half, half),
        in_specs=[smem_spec(), smem_spec()] + [any_spec()] * 5,
        out_specs=(vmem_spec(), vmem_spec()),
        scratch_shapes=[pltpu.SemaphoreType.DMA((8,))],
        name="take_far",
    )(place, slots, *items)


def take_near(place, up_slots, down_slots, items, passing, axes, width):
    def kernel(place_ref, up_ref, down_ref, *refs):
        item_refs, (pass_up, pass_down), (to_up, to_down), sems = refs[:5], refs[5:7], refs[7:9], refs[9]
        coords = coords_of(place_ref)
        reduce_axis = axes[2]
        for i in range(8):
            for which, (slot_ref, out) in enumerate(((up_ref, to_up), (down_ref, to_down))):
                slot = slot_ref[i]
                sem = sems.at[which, i]
                target = out.at[i]
                if (i < 4) == (which == 0):
                    mine = field(slot, reduce_axis) == coords[reduce_axis]
                    through = (pass_up if which == 0 else pass_down).at[i % 4]

                    @pl.when(mine)
                    def _():
                        start_item(slot, coords, axes, item_refs, target, sem)

                    @pl.when(jnp.logical_not(mine))
                    def _():
                        pltpu.make_async_copy(through, target, sem).start()

                else:
                    start_item(slot, coords, axes, item_refs, target, sem)
        for i in range(8):
            for which, out in enumerate((to_up, to_down)):
                pltpu.make_async_copy(item_refs[0].at[0], out.at[i], sems.at[which, i]).wait()

    full = jax.ShapeDtypeStruct((8, RANK, width), jnp.bfloat16)
    return pl.pallas_call(
        kernel,
        out_shape=(full, full),
        in_specs=[smem_spec()] * 3 + [any_spec()] * 7,
        out_specs=(vmem_spec(), vmem_spec()),
        scratch_shapes=[pltpu.SemaphoreType.DMA((2, 8))],
        name="take_near",
    )(place, up_slots, down_slots, *items, *passing)


def take_own(place, slots, items, axes, width):
    def kernel(place_ref, slot_ref, *refs):
        item_refs, out, sems = refs[:5], refs[5], refs[6]
        coords = coords_of(place_ref)
        for i in range(8):
            start_item(slot_ref[i], coords, axes, item_refs, out.at[i], sems.at[i])
        for i in range(8):
            pltpu.make_async_copy(item_refs[0].at[0], out.at[i], sems.at[i]).wait()

    return pl.pallas_call(
        kernel,
        out_shape=jax.ShapeDtypeStruct((8, RANK, width), jnp.bfloat16),
        in_specs=[smem_spec()] * 2 + [any_spec()] * 5,
        out_specs=vmem_spec(),
        scratch_shapes=[pltpu.SemaphoreType.DMA((8,))],
        name="take_own",
    )(place, slots, *items)


def start_arrived(i, slot, coords, axis, sources, lanes, target, sem):
    rel = (field(slot, axis) - coords[axis]) & 3
    own, below, above = sources
    is_own = rel == 0
    is_below = (rel != 0) & (rel != 1) if i < 4 else rel == 3
    is_above = rel == 1 if i < 4 else (rel != 0) & (rel != 3)
    for flag, ref in ((is_own, own), (is_below, below), (is_above, above)):

        @pl.when(flag)
        def _(ref=ref):
            pltpu.make_async_copy(ref.at[i, :, lanes], target, sem).start()


def segments(index, ends_ref):
    total = jnp.zeros_like(index)
    for p in range(8):
        total = total + (index >= ends_ref[p]).astype(jnp.int32)
    return total


def rank_part(place, slots, ends, features, arrived, width):
    tok, feat = features.shape
    axis = AXES[0][2]

    def kernel(place_ref, slot_ref, ends_ref, feat_ref, own, below, above, out_ref, down, sems):
        coords = coords_of(place_ref)
        for i in range(8):
            start_arrived(
                i, slot_ref[i], coords, axis, (own, below, above), pl.ds(0, feat), down.at[pl.ds(i * RANK, RANK)], sems.at[i]
            )
        for i in range(8):
            pltpu.make_async_copy(own.at[0, :, pl.ds(0, feat)], down.at[pl.ds(i * RANK, RANK)], sems.at[i]).wait()
        proj = lax.dot_general(feat_ref[...], down[...], (((1,), (1,)), ((), ())), preferred_element_type=jnp.float32)
        rows = lax.broadcasted_iota(jnp.int32, proj.shape, 0)
        cols = lax.broadcasted_iota(jnp.int32, proj.shape, 1)
        out_ref[...] = jnp.where(segments(rows, ends_ref) == (cols >> 4), proj, 0.0)

    return pl.pallas_call(
        kernel,
        out_shape=jax.ShapeDtypeStruct((tok, 8 * RANK), jnp.float32),
        in_specs=[smem_spec()] * 3 + [pl.BlockSpec((tok, feat), lambda: (0, 0))] + [any_spec()] * 3,
        out_specs=pl.BlockSpec((tok, 8 * RANK), lambda: (0, 0)),
        scratch_shapes=[pltpu.VMEM((8 * RANK, feat), jnp.bfloat16), pltpu.SemaphoreType.DMA((8,))],
        name="rank_part",
    )(place, slots, ends, features, *arrived)


def project(normed, weight, which):
    tok, width = normed.shape
    cols = weight.shape[2]
    tile = 512

    def kernel(x_ref, w_ref, o_ref):
        o_ref[...] = jnp.dot(x_ref[...], w_ref[...], preferred_element_type=jnp.float32)

    return pl.pallas_call(
        kernel,
        out_shape=jax.ShapeDtypeStruct((tok, cols), jnp.float32),
        grid=(cols // tile,),
        in_specs=[
            pl.BlockSpec((tok, width), lambda n: (0, 0)),
            pl.BlockSpec((None, width, tile), lambda n: (which, 0, n)),
        ],
        out_specs=pl.BlockSpec((tok, tile), lambda n: (0, n)),
        name="project",
        cost_estimate=pl.CostEstimate(
            flops=2 * tok * width * cols, transcendentals=0, bytes_accessed=2 * width * cols + 2 * tok * width + 4 * tok * cols
        ),
    )(normed, weight)


def tail(place, slots, ends, slopes, act, act_other, base, arrived, out_weight, heads, splits, widths):
    tok = act.shape[0]
    cols = base[0].shape[1]
    model = out_weight.shape[1]
    scale = 1.0 / math.sqrt(HEAD_DIM)
    half = tok // 2
    chunk = 4
    up_widths = [3 * HEAD_DIM * n for n in splits]
    skips = [w - u for w, u in zip(widths, up_widths)]
    firsts = [sum(splits[:p]) for p in range(3)]
    rows_w = cols // chunk

    def kernel(place_ref, slot_ref, ends_ref, slope_ref, act_ref, other_ref, *refs):
        base_hbm, arrived_refs, w_hbm = refs[:3], refs[3:12], refs[12]
        keep_ref, send_ref = refs[13:15]
        ups, base_buf, w_buf, att, up_sems, base_sems, w_sems = refs[15:18], *refs[18:24]
        coords = coords_of(place_ref)
        for p in range(3):
            for i in range(8):
                start_arrived(
                    i,
                    slot_ref[i],
                    coords,
                    AXES[p][2],
                    arrived_refs[3 * p : 3 * p + 3],
                    pl.ds(skips[p], up_widths[p]),
                    ups[p].at[pl.ds(i * RANK, RANK)],
                    up_sems.at[p, i],
                )

        def base_copy(p, j):
            lanes = pl.ds(firsts[p] * HEAD_DIM, splits[p] * HEAD_DIM)
            return pltpu.make_async_copy(base_hbm[j].at[:, lanes], base_buf.at[j, :, lanes], base_sems.at[p, j])

        def w_copy(k):
            rows = pl.ds(k * rows_w, rows_w)
            return pltpu.make_async_copy(w_hbm.at[rows], w_buf.at[rows], w_sems.at[k])

        for p in range(3):
            for j in range(3):
                base_copy(p, j).start()
        for k in range(chunk):
            w_copy(k).start()

        rows = lax.broadcasted_iota(jnp.int32, (tok, 128), 0)
        starts = jnp.maximum((rows >> 6) * 64 - 64, 0)
        keys_at = lax.broadcasted_iota(jnp.int32, (tok, 128), 1) + starts
        allowed = (segments(rows, ends_ref) == segments(keys_at, ends_ref)) & (keys_at <= rows)
        apart = (keys_at - rows).astype(jnp.float32)
        low = (act_ref[...] + other_ref[...]).astype(jnp.bfloat16)
        core = place_ref[3]
        for p in range(3):
            for i in range(8):
                pltpu.make_async_copy(
                    arrived_refs[3 * p].at[0, :, pl.ds(skips[p], up_widths[p])],
                    ups[p].at[pl.ds(i * RANK, RANK)],
                    up_sems.at[p, i],
                ).wait()
            for j in range(3):
                base_copy(p, j).wait()
            for t in range(splits[p]):
                h = firsts[p] + t
                mine = []
                for j in range(3):
                    at = (j * splits[p] + t) * HEAD_DIM
                    delta = jnp.dot(low, ups[p][:, at : at + HEAD_DIM], preferred_element_type=jnp.float32)
                    delta = delta.astype(jnp.bfloat16).astype(jnp.float32)
                    whole = base_buf[j, :, h * HEAD_DIM : (h + 1) * HEAD_DIM] + LOWRANK_SCALE * delta
                    mine.append(whole.astype(jnp.bfloat16))
                q, k, v = mine
                blocks = []
                for b in range(4):
                    w0 = max(64 * b - 64, 0)
                    blocks.append(
                        lax.dot_general(
                            q[64 * b : 64 * b + 64],
                            k[w0 : w0 + 128],
                            (((1,), (1,)), ((), ())),
                            preferred_element_type=jnp.float32,
                        )
                    )
                s = jnp.concatenate(blocks, 0)
                s = jnp.where(allowed, s * scale + slope_ref[h] * apart, -jnp.inf)
                e = jnp.exp(s - jnp.max(s, -1, keepdims=True))
                pr = (e / jnp.sum(e, -1, keepdims=True)).astype(jnp.bfloat16)
                outs = []
                for b in range(4):
                    w0 = max(64 * b - 64, 0)
                    outs.append(
                        jnp.dot(pr[64 * b : 64 * b + 64], v[w0 : w0 + 128], preferred_element_type=jnp.float32)
                    )
                o = jnp.concatenate(outs, 0).astype(jnp.bfloat16)
                lanes = slice(h * HEAD_DIM, (h + 1) * HEAD_DIM)
                for m in range(2):
                    at = pl.multiple_of(((core + m) & 1) * half, half)
                    att[pl.ds(at, half), lanes] = o[m * half : (m + 1) * half]
        for k in range(chunk):
            w_copy(k).wait()
        n_tile = 512
        for n in range(model // n_tile):
            lanes = slice(n * n_tile, (n + 1) * n_tile)
            part = jnp.dot(att[...], w_buf[:, lanes], preferred_element_type=jnp.float32).astype(jnp.bfloat16)
            keep_ref[:, lanes] = part[:half]
            send_ref[:, lanes] = part[half:]

    half_out = jax.ShapeDtypeStruct((half, model), jnp.bfloat16)
    return pl.pallas_call(
        kernel,
        out_shape=(half_out, half_out),
        in_specs=[smem_spec()] * 4
        + [pl.BlockSpec((tok, 8 * RANK), lambda: (0, 0))] * 2
        + [any_spec()] * 13,
        out_specs=(pl.BlockSpec((half, model), lambda: (0, 0)),) * 2,
        scratch_shapes=[pltpu.VMEM((8 * RANK, w), jnp.bfloat16) for w in up_widths]
        + [
            pltpu.VMEM((3, tok, cols), jnp.float32),
            pltpu.VMEM((cols, model), jnp.bfloat16),
            pltpu.VMEM((tok, cols), jnp.bfloat16),
            pltpu.SemaphoreType.DMA((3, 8)),
            pltpu.SemaphoreType.DMA((3, 3)),
            pltpu.SemaphoreType.DMA((chunk,)),
        ],
        name="tail",
        compiler_params=pltpu.CompilerParams(vmem_limit_bytes=50 * 1024 * 1024),
    )(place, slots, ends, slopes, act, act_other, *base, *[a for part in arrived for a in part], out_weight)


def on_device(
    tokens,
    layer_norm_gain,
    query_key_value_weight,
    output_weight,
    stored_down_weight,
    stored_up_weight,
    group_prompt_length,
    prompt_adapter_index,
    placement,
):
    tok_count, width = tokens.shape
    tp_index = lax.axis_index("tp")
    req_index = lax.axis_index("req")
    head_part = query_key_value_weight.shape[2]
    local_heads = head_part // HEAD_DIM
    half = tok_count // 2

    table = jnp.arange(placement.shape[0], dtype=jnp.int32)
    slots = jnp.sum(
        jnp.where(table[None, :] == prompt_adapter_index[0][:, None], placement[None, :], 0), 1
    ).astype(jnp.int32)
    place = jnp.stack([req_index & 3, (req_index >> 2) & 3, (req_index >> 4) & 3, tp_index]).astype(jnp.int32)
    ends = jnp.cumsum(group_prompt_length[0]).astype(jnp.int32)

    down = jnp.transpose(stored_down_weight, (0, 2, 1))
    splits = (2, 7, 7)
    info = jnp.broadcast_to(
        jnp.pad(slots.astype(jnp.bfloat16), (0, INFO - 8))[None, None, :], (4, RANK, INFO)
    )
    own, widths, first = [], [], 0
    for p, n in enumerate(splits):
        lanes = slice(first * HEAD_DIM, (first + n) * HEAD_DIM)
        pieces = [stored_up_weight[:, :, j, lanes] for j in range(3)]
        own.append(jnp.concatenate(([down] if p == 0 else []) + pieces + [info], -1))
        widths.append(own[-1].shape[2] - INFO)
        first += n

    below1, above1, far1 = {}, {}, {}
    for p in range(3):
        axis = AXES[p][0]
        far1[p] = shift(own[p], axis, 2)
        below1[p] = shift(own[p], axis, 1)
        above1[p] = shift(own[p], axis, -1)

    def asked(array, w):
        return array[0, 0, w : w + 8].astype(jnp.int32)

    wide = tokens.astype(jnp.float32)
    mean = jnp.mean(wide, -1, keepdims=True)
    centred = wide - mean
    variance = jnp.mean(centred * centred, -1, keepdims=True)
    normed = (centred * lax.rsqrt(variance + EPS) * layer_norm_gain.astype(jnp.float32)).astype(jnp.bfloat16)
    features = lax.dynamic_slice_in_dim(normed, tp_index * head_part, head_part, 1)
    weight = jnp.transpose(query_key_value_weight, (1, 0, 2))
    base = [project(normed, weight, j) for j in range(3)]

    gathered = []
    for p in range(3):
        w = widths[p]
        gathered.append(jnp.concatenate([a[:, :, :w] for a in (own[p], above1[p], far1[p], below1[p])], 0))
    below2 = [shift(gathered[p], AXES[p][1], 1) for p in range(3)]
    above2 = [shift(gathered[p], AXES[p][1], -1) for p in range(3)]
    far_lo = [shift(below2[p][:8], AXES[p][1], 1) for p in range(3)]
    far_hi = [shift(above2[p][8:], AXES[p][1], -1) for p in range(3)]

    arrived = []
    for p in range(3):
        axes = AXES[p]
        w = widths[p]
        items = (gathered[p], below2[p], above2[p], far_lo[p], far_hi[p])
        (giver,) = [g for g in range(3) if AXES[g][0] == axes[2]]
        gw = widths[giver]
        t_up, t_down = take_far(place, asked(far1[giver], gw), items, axes, w)
        pass_up = shift(t_up, axes[2], 1)
        pass_down = shift(t_down, axes[2], -1)
        mine = take_own(place, slots, items, axes, w)
        s_up, s_down = take_near(
            place, asked(above1[giver], gw), asked(below1[giver], gw), items, (pass_up, pass_down), axes, w
        )
        arrived.append((mine, shift(s_up, axes[2], 1), shift(s_down, axes[2], -1)))

    swap = [(0, 1), (1, 0)]
    act = rank_part(place, slots, ends, features, arrived[0], widths[0])
    act_other = lax.ppermute(act, "tp", swap)
    head_ids = tp_index * local_heads + jnp.arange(local_heads, dtype=jnp.int32)
    slopes = jnp.exp2(-8.0 * (head_ids.astype(jnp.float32) + 1.0) / HEADS)
    keep, send = tail(
        place, slots, ends, slopes, act, act_other, base, arrived, output_weight, local_heads, splits, widths
    )
    got = lax.ppermute(send, "tp", swap)
    residual = lax.dynamic_slice_in_dim(tokens, tp_index * half, half, 0)
    return (keep.astype(jnp.float32) + got.astype(jnp.float32) + residual.astype(jnp.float32)).astype(jnp.bfloat16)


def solution(mesh):
    in_specs = (
        P("req", None),
        P(),
        P(None, None, "tp"),
        P("tp", None),
        P("req", "tp", None),
        P("req", None, None, "tp"),
        P("req", None),
        P("req", None),
        P(),
    )
    out_specs = P(("req", "tp"), None)
    return jax.shard_map(on_device, mesh=mesh, in_specs=in_specs, out_specs=out_specs, check_vma=False)
```

```python
import math

import jax
import jax.numpy as jnp
from jax import lax
from jax.experimental import pallas as pl
from jax.experimental.pallas import tpu as pltpu
from jax.sharding import PartitionSpec as P

HEADS = 32
HEAD_DIM = 128
LOWRANK_SCALE = 0.5
EPS = 1e-05
RANK = 16
SIDE = 4
STRIDE = {"x": 1, "y": SIDE, "z": SIDE * SIDE}
SHIFT = {"x": 2, "y": 4, "z": 6}
AXES = (("z", "y", "x"), ("x", "z", "y"), ("y", "x", "z"))
INFO = 128


def ring(axis, step):
    stride = STRIDE[axis]
    pairs = []
    for r in range(SIDE**3):
        c = (r // stride) % SIDE
        pairs.append((r, r + ((c + step) % SIDE - c) * stride))
    return pairs


def shift(value, axis, step):
    return lax.ppermute(value, "req", ring(axis, step))


def field(slot, axis):
    return (slot >> SHIFT[axis]) & (SIDE - 1)


def copy_item(slot, coords, axes, items, store):
    a, b, _ = axes
    own, below, above, far0, far1 = items
    rel_a = (field(slot, a) - coords[a]) & 3
    rel_b = (field(slot, b) - coords[b]) & 3
    row = rel_a * 4 + (slot & 3)
    for flag, ref, at in (
        (rel_b == 0, own, row),
        (rel_b == 3, below, row),
        (rel_b == 1, above, row),
        ((rel_b == 2) & (row < 8), far0, row & 7),
        ((rel_b == 2) & (row >= 8), far1, row & 7),
    ):

        @pl.when(flag)
        def _(ref=ref, at=at):
            store(ref[at])


def coords_of(ref):
    return {"x": ref[0], "y": ref[1], "z": ref[2]}


def any_spec():
    return pl.BlockSpec(memory_space=pl.ANY)


def vmem_spec():
    return pl.BlockSpec(memory_space=pltpu.VMEM)


def smem_spec():
    return pl.BlockSpec(memory_space=pltpu.SMEM)


def small(mib):
    return pltpu.CompilerParams(vmem_limit_bytes=mib * 1024 * 1024)


def take_far(place, asked, which, items, axes, width):
    def kernel(place_ref, asked_ref, *refs):
        item_refs, (lo, hi) = refs[:5], refs[5:7]
        coords = coords_of(place_ref)
        for i in range(8):
            out = lo if i < 4 else hi

            def store(value, out=out, i=i):
                out[i % 4] = value

            copy_item(asked_ref[which, i], coords, axes, item_refs, store)

    half = jax.ShapeDtypeStruct((4, RANK, width), jnp.bfloat16)
    return pl.pallas_call(
        kernel,
        out_shape=(half, half),
        in_specs=[smem_spec(), smem_spec()] + [vmem_spec()] * 5,
        out_specs=(vmem_spec(), vmem_spec()),
        name="take_far",
        compiler_params=small(12),
    )(place, asked, *items)


def take_near(place, slots, asked, which_up, which_down, items, passing, axes, width):
    def kernel(place_ref, slot_ref, asked_ref, *refs):
        item_refs, (pass_up, pass_down), (to_up, to_down, own) = refs[:5], refs[5:7], refs[7:10]
        coords = coords_of(place_ref)
        for i in range(8):
            for which, through, out in ((which_up, pass_up, to_up), (which_down, pass_down, to_down)):
                slot = asked_ref[which, i]

                def store(value, out=out, i=i):
                    out[i] = value

                if (i < 4) == (out is to_up):
                    mine = field(slot, axes[2]) == coords[axes[2]]

                    @pl.when(mine)
                    def _(slot=slot, store=store):
                        copy_item(slot, coords, axes, item_refs, store)

                    @pl.when(jnp.logical_not(mine))
                    def _(through=through, store=store, i=i):
                        store(through[i % 4])

                else:
                    copy_item(slot, coords, axes, item_refs, store)

            def store_own(value, i=i):
                own[i] = value

            copy_item(slot_ref[i], coords, axes, item_refs, store_own)

    full = jax.ShapeDtypeStruct((8, RANK, width), jnp.bfloat16)
    return pl.pallas_call(
        kernel,
        out_shape=(full, full, full),
        in_specs=[smem_spec()] * 3 + [vmem_spec()] * 7,
        out_specs=(vmem_spec(),) * 3,
        name="take_near",
        compiler_params=small(16),
    )(place, slots, asked, *items, *passing)


def copy_arrived(i, slot, coords, axis, sources, store):
    rel = (field(slot, axis) - coords[axis]) & 3
    own, below, above = sources
    is_below = (rel != 0) & (rel != 1) if i < 4 else rel == 3
    is_above = rel == 1 if i < 4 else (rel != 0) & (rel != 3)
    for flag, ref in ((rel == 0, own), (is_below, below), (is_above, above)):

        @pl.when(flag)
        def _(ref=ref):
            store(ref)


def segments(index, length_ref):
    total = jnp.zeros_like(index)
    end = length_ref[0, 0]
    for p in range(8):
        total = total + (index >= end).astype(jnp.int32)
        if p < 7:
            end = end + length_ref[0, p + 1]
    return total


def pack(down, up, chosen, placement, splits, widths):
    firsts = [sum(splits[:p]) for p in range(3)]

    def kernel(chosen_ref, place_ref, down_hbm, up_hbm, *refs):
        parts, slot_ref, sems = refs[:3], refs[3], refs[4]
        copies = []

        def go(source, target):
            copies.append(pltpu.make_async_copy(source, target, sems.at[len(copies)]))
            copies[-1].start()

        go(down_hbm, parts[0].at[:, :, pl.ds(0, down.shape[2])])
        for p in range(3):
            wide = splits[p] * HEAD_DIM
            at = widths[p] - 3 * wide
            for j in range(3):
                go(up_hbm.at[:, j, :, pl.ds(firsts[p] * HEAD_DIM, wide)], parts[p].at[:, :, pl.ds(at + j * wide, wide)])
        lane = lax.broadcasted_iota(jnp.int32, (RANK, INFO), 1)
        note = jnp.zeros((RANK, INFO), jnp.int32)
        for i in range(8):
            slot = place_ref[chosen_ref[0, i]]
            slot_ref[i] = slot
            note = jnp.where(lane == i, slot, note)
        note = note.astype(jnp.float32).astype(jnp.bfloat16)
        for p in range(3):
            for k in range(4):
                parts[p][k, :, widths[p] :] = note
        for c in copies:
            c.wait()

    return pl.pallas_call(
        kernel,
        out_shape=tuple(jax.ShapeDtypeStruct((4, RANK, w + INFO), jnp.bfloat16) for w in widths)
        + (jax.ShapeDtypeStruct((8,), jnp.int32),),
        in_specs=[smem_spec(), smem_spec(), any_spec(), any_spec()],
        out_specs=(vmem_spec(),) * 3 + (smem_spec(),),
        scratch_shapes=[pltpu.SemaphoreType.DMA((10,))],
        name="pack",
        compiler_params=small(8),
    )(chosen, placement, down, up)


def rank_part(place, slots, lengths, normed, arrived, feat):
    tok = normed.shape[0]
    axis = AXES[0][2]

    def kernel(place_ref, slot_ref, length_ref, x_ref, own, below, above, out_ref, down):
        coords = coords_of(place_ref)
        for i in range(8):

            def store(ref, i=i):
                down[i * RANK : (i + 1) * RANK, :] = ref[i, :, 0:feat]

            copy_arrived(i, slot_ref[i], coords, axis, (own, below, above), store)
        mine = x_ref[:, pl.ds(pl.multiple_of(place_ref[3] * feat, feat), feat)]
        proj = lax.dot_general(mine, down[...], (((1,), (1,)), ((), ())), preferred_element_type=jnp.float32)
        rows = lax.broadcasted_iota(jnp.int32, proj.shape, 0)
        cols = lax.broadcasted_iota(jnp.int32, proj.shape, 1)
        out_ref[...] = jnp.where(segments(rows, length_ref) == (cols >> 4), proj, 0.0)

    return pl.pallas_call(
        kernel,
        out_shape=jax.ShapeDtypeStruct((tok, 8 * RANK), jnp.float32),
        in_specs=[smem_spec()] * 3 + [vmem_spec()] * 4,
        out_specs=vmem_spec(),
        scratch_shapes=[pltpu.VMEM((8 * RANK, feat), jnp.bfloat16)],
        name="rank_part",
        compiler_params=small(12),
    )(place, slots, lengths, normed, *arrived)


def project(normed, weight, which):
    tok, width = normed.shape
    cols = weight.shape[2]
    tile = 512

    def kernel(x_ref, w_ref, o_ref):
        o_ref[...] = jnp.dot(x_ref[...], w_ref[...], preferred_element_type=jnp.float32)

    return pl.pallas_call(
        kernel,
        out_shape=jax.ShapeDtypeStruct((tok, cols), jnp.float32),
        grid=(cols // tile,),
        in_specs=[
            pl.BlockSpec((tok, width), lambda n: (0, 0)),
            pl.BlockSpec((None, width, tile), lambda n: (which, 0, n)),
        ],
        out_specs=pl.BlockSpec((tok, tile), lambda n: (0, n)),
        name="project",
        compiler_params=small(20),
        cost_estimate=pl.CostEstimate(
            flops=2 * tok * width * cols, transcendentals=0, bytes_accessed=2 * width * cols + 2 * tok * width + 4 * tok * cols
        ),
    )(normed, weight)


def tail(place, slots, lengths, slopes, act, act_other, base, arrived, out_weight, heads, splits, widths):
    tok = act.shape[0]
    cols = base[0].shape[1]
    model = out_weight.shape[1]
    scale = 1.0 / math.sqrt(HEAD_DIM)
    half = tok // 2
    chunk = 4
    rows_w = cols // chunk
    up_widths = [3 * HEAD_DIM * n for n in splits]
    skips = [w - u for w, u in zip(widths, up_widths)]
    firsts = [sum(splits[:p]) for p in range(3)]

    def kernel(place_ref, slot_ref, length_ref, slope_ref, act_ref, other_ref, *refs):
        base_refs, arrived_refs, w_ref = refs[:3], refs[3:12], refs[12]
        keep_ref, send_ref = refs[13:15]
        ups, (att, base_buf, w_buf, base_sems, w_sems) = refs[15:18], refs[18:23]
        coords = coords_of(place_ref)

        def base_copy(p, j):
            lanes = pl.ds(firsts[p] * HEAD_DIM, splits[p] * HEAD_DIM)
            return pltpu.make_async_copy(base_refs[j].at[:, lanes], base_buf.at[j, :, lanes], base_sems.at[p, j])

        def w_copy(k):
            rows = pl.ds(k * rows_w, rows_w)
            return pltpu.make_async_copy(w_ref.at[rows], w_buf.at[rows], w_sems.at[k])

        for p in range(3):
            for j in range(3):
                base_copy(p, j).start()
        for k in range(chunk):
            w_copy(k).start()
        for p in range(3):
            for i in range(8):

                def store(ref, p=p, i=i):
                    ups[p][i * RANK : (i + 1) * RANK, :] = ref[i, :, skips[p] :]

                copy_arrived(i, slot_ref[i], coords, AXES[p][2], arrived_refs[3 * p : 3 * p + 3], store)
        rows = lax.broadcasted_iota(jnp.int32, (tok, 128), 0)
        starts = jnp.maximum((rows >> 6) * 64 - 64, 0)
        keys_at = lax.broadcasted_iota(jnp.int32, (tok, 128), 1) + starts
        allowed = (segments(rows, length_ref) == segments(keys_at, length_ref)) & (keys_at <= rows)
        apart = (keys_at - rows).astype(jnp.float32)
        low = (act_ref[...] + other_ref[...]).astype(jnp.bfloat16)
        core = place_ref[3]
        for p in range(3):
            for j in range(3):
                base_copy(p, j).wait()
            for t in range(splits[p]):
                h = firsts[p] + t
                mine = []
                for j in range(3):
                    at = (j * splits[p] + t) * HEAD_DIM
                    delta = jnp.dot(low, ups[p][:, at : at + HEAD_DIM], preferred_element_type=jnp.float32)
                    delta = delta.astype(jnp.bfloat16).astype(jnp.float32)
                    whole = base_buf[j, :, h * HEAD_DIM : (h + 1) * HEAD_DIM] + LOWRANK_SCALE * delta
                    mine.append(whole.astype(jnp.bfloat16))
                q, k, v = mine
                blocks = []
                for b in range(4):
                    w0 = max(64 * b - 64, 0)
                    blocks.append(
                        lax.dot_general(
                            q[64 * b : 64 * b + 64],
                            k[w0 : w0 + 128],
                            (((1,), (1,)), ((), ())),
                            preferred_element_type=jnp.float32,
                        )
                    )
                s = jnp.concatenate(blocks, 0)
                s = jnp.where(allowed, s * scale + slope_ref[h] * apart, -jnp.inf)
                e = jnp.exp(s - jnp.max(s, -1, keepdims=True))
                pr = (e / jnp.sum(e, -1, keepdims=True)).astype(jnp.bfloat16)
                outs = []
                for b in range(4):
                    w0 = max(64 * b - 64, 0)
                    outs.append(
                        jnp.dot(pr[64 * b : 64 * b + 64], v[w0 : w0 + 128], preferred_element_type=jnp.float32)
                    )
                o = jnp.concatenate(outs, 0).astype(jnp.bfloat16)
                lanes = slice(h * HEAD_DIM, (h + 1) * HEAD_DIM)
                for m in range(2):
                    at = pl.multiple_of(((core + m) & 1) * half, half)
                    att[pl.ds(at, half), lanes] = o[m * half : (m + 1) * half]
        for k in range(chunk):
            w_copy(k).wait()
        n_tile = 512
        for n in range(model // n_tile):
            lanes = slice(n * n_tile, (n + 1) * n_tile)
            part = jnp.dot(att[...], w_buf[:, lanes], preferred_element_type=jnp.float32).astype(jnp.bfloat16)
            keep_ref[:, lanes] = part[:half]
            send_ref[:, lanes] = part[half:]

    half_out = jax.ShapeDtypeStruct((half, model), jnp.bfloat16)
    return pl.pallas_call(
        kernel,
        out_shape=(half_out, half_out),
        in_specs=[smem_spec()] * 4 + [vmem_spec()] * 2 + [any_spec()] * 3 + [vmem_spec()] * 9 + [any_spec()],
        out_specs=(vmem_spec(),) * 2,
        scratch_shapes=[pltpu.VMEM((8 * RANK, w), jnp.bfloat16) for w in up_widths]
        + [
            pltpu.VMEM((tok, cols), jnp.bfloat16),
            pltpu.VMEM((3, tok, cols), jnp.float32),
            pltpu.VMEM((cols, model), jnp.bfloat16),
            pltpu.SemaphoreType.DMA((3, 3)),
            pltpu.SemaphoreType.DMA((chunk,)),
        ],
        name="tail",
        compiler_params=pltpu.CompilerParams(vmem_limit_bytes=44 * 1024 * 1024),
    )(place, slots, lengths, slopes, act, act_other, *base, *[a for part in arrived for a in part], out_weight)


def on_device(
    tokens,
    layer_norm_gain,
    query_key_value_weight,
    output_weight,
    stored_down_weight,
    stored_up_weight,
    group_prompt_length,
    prompt_adapter_index,
    placement,
):
    tok_count, width = tokens.shape
    tp_index = lax.axis_index("tp")
    req_index = lax.axis_index("req")
    head_part = query_key_value_weight.shape[2]
    local_heads = head_part // HEAD_DIM
    half = tok_count // 2

    place = jnp.stack([req_index & 3, (req_index >> 2) & 3, (req_index >> 4) & 3, tp_index]).astype(jnp.int32)

    down = jnp.transpose(stored_down_weight, (0, 2, 1))
    up = jnp.transpose(stored_up_weight, (0, 2, 1, 3))
    splits = (2, 7, 7)
    widths = [3 * HEAD_DIM * n + (head_part if p == 0 else 0) for p, n in enumerate(splits)]
    *own, slots = pack(down, up, prompt_adapter_index, placement, splits, widths)

    below1, above1, far1 = {}, {}, {}
    for p in range(3):
        axis = AXES[p][0]
        far1[p] = shift(own[p], axis, 2)
        below1[p] = shift(own[p], axis, 1)
        above1[p] = shift(own[p], axis, -1)

    asked = jnp.stack(
        [a[0, 0, widths[p] : widths[p] + 8] for p in range(3) for a in (far1[p], above1[p], below1[p])]
    ).astype(jnp.int32)

    wide = tokens.astype(jnp.float32)
    mean = jnp.mean(wide, -1, keepdims=True)
    centred = wide - mean
    variance = jnp.mean(centred * centred, -1, keepdims=True)
    normed = (centred * lax.rsqrt(variance + EPS) * layer_norm_gain.astype(jnp.float32)).astype(jnp.bfloat16)
    weight = jnp.transpose(query_key_value_weight, (1, 0, 2))
    base = [project(normed, weight, j) for j in range(3)]

    gathered = []
    for p in range(3):
        w = widths[p]
        gathered.append(jnp.concatenate([a[:, :, :w] for a in (own[p], above1[p], far1[p], below1[p])], 0))
    below2 = [shift(gathered[p], AXES[p][1], 1) for p in range(3)]
    above2 = [shift(gathered[p], AXES[p][1], -1) for p in range(3)]
    below2, above2, base[0], base[1] = lax.optimization_barrier((below2, above2, base[0], base[1]))
    far_lo = [shift(below2[p][:8], AXES[p][1], 1) for p in range(3)]
    far_hi = [shift(above2[p][8:], AXES[p][1], -1) for p in range(3)]

    arrived = []
    for p in range(3):
        axes = AXES[p]
        w = widths[p]
        items = (gathered[p], below2[p], above2[p], far_lo[p], far_hi[p])
        (giver,) = [g for g in range(3) if AXES[g][0] == axes[2]]
        t_up, t_down = take_far(place, asked, 3 * giver, items, axes, w)
        passing = (shift(t_up, axes[2], 1), shift(t_down, axes[2], -1))
        if p == 0:
            *passing, base[2] = lax.optimization_barrier((*passing, base[2]))
        s_up, s_down, mine = take_near(
            place, slots, asked, 3 * giver + 1, 3 * giver + 2, items, passing, axes, w
        )
        arrived.append((mine, shift(s_up, axes[2], 1), shift(s_down, axes[2], -1)))

    swap = [(0, 1), (1, 0)]
    act = rank_part(place, slots, group_prompt_length, normed, arrived[0], head_part)
    act_other = lax.ppermute(act, "tp", swap)
    head_ids = tp_index * local_heads + jnp.arange(local_heads, dtype=jnp.int32)
    slopes = jnp.exp2(-8.0 * (head_ids.astype(jnp.float32) + 1.0) / HEADS)
    keep, send = tail(
        place, slots, group_prompt_length, slopes, act, act_other, base, arrived, output_weight, local_heads, splits, widths
    )
    got = lax.ppermute(send, "tp", swap)
    residual = lax.dynamic_slice_in_dim(tokens, tp_index * half, half, 0)
    return (keep.astype(jnp.float32) + got.astype(jnp.float32) + residual.astype(jnp.float32)).astype(jnp.bfloat16)


def solution(mesh):
    in_specs = (
        P("req", None),
        P(),
        P(None, None, "tp"),
        P("tp", None),
        P("req", "tp", None),
        P("req", None, None, "tp"),
        P("req", None),
        P("req", None),
        P(),
    )
    out_specs = P(("req", "tp"), None)
    return jax.shard_map(on_device, mesh=mesh, in_specs=in_specs, out_specs=out_specs, check_vma=False)
```

```python
import math

import jax
import jax.numpy as jnp
from jax import lax
from jax.experimental import pallas as pl
from jax.experimental.pallas import tpu as pltpu
from jax.sharding import PartitionSpec as P

HEADS = 32
HEAD_DIM = 128
LOWRANK_SCALE = 0.5
EPS = 1e-05
RANK = 16
SIDE = 4
STRIDE = {"x": 1, "y": SIDE, "z": SIDE * SIDE}
SHIFT = {"x": 2, "y": 4, "z": 6}
AXES = (("z", "y", "x"), ("x", "z", "y"), ("y", "x", "z"))
INFO = 128


def ring(axis, step):
    stride = STRIDE[axis]
    pairs = []
    for r in range(SIDE**3):
        c = (r // stride) % SIDE
        pairs.append((r, r + ((c + step) % SIDE - c) * stride))
    return pairs


def shift(value, axis, step):
    return lax.ppermute(value, "req", ring(axis, step))


def field(slot, axis):
    return (slot >> SHIFT[axis]) & (SIDE - 1)


def copy_item(slot, coords, axes, items, store):
    a, b, _ = axes
    own, below, above, far0, far1 = items
    rel_a = (field(slot, a) - coords[a]) & 3
    rel_b = (field(slot, b) - coords[b]) & 3
    row = rel_a * 4 + (slot & 3)
    for flag, ref, at in (
        (rel_b == 0, own, row),
        (rel_b == 3, below, row),
        (rel_b == 1, above, row),
        ((rel_b == 2) & (row < 8), far0, row & 7),
        ((rel_b == 2) & (row >= 8), far1, row & 7),
    ):

        @pl.when(flag)
        def _(ref=ref, at=at):
            store(ref[at])


def coords_of(ref):
    return {"x": ref[0], "y": ref[1], "z": ref[2]}


def any_spec():
    return pl.BlockSpec(memory_space=pl.ANY)


def vmem_spec():
    return pl.BlockSpec(memory_space=pltpu.VMEM)


def smem_spec():
    return pl.BlockSpec(memory_space=pltpu.SMEM)


def small(mib):
    return pltpu.CompilerParams(vmem_limit_bytes=mib * 1024 * 1024)


def take_far(place, asked, which, items, axes, width):
    def kernel(place_ref, asked_ref, *refs):
        item_refs, (lo, hi) = refs[:5], refs[5:7]
        coords = coords_of(place_ref)
        for i in range(8):
            out = lo if i < 4 else hi

            def store(value, out=out, i=i):
                out[i % 4] = value

            copy_item(asked_ref[which, i], coords, axes, item_refs, store)

    half = jax.ShapeDtypeStruct((4, RANK, width), jnp.bfloat16)
    return pl.pallas_call(
        kernel,
        out_shape=(half, half),
        in_specs=[smem_spec(), smem_spec()] + [vmem_spec()] * 5,
        out_specs=(vmem_spec(), vmem_spec()),
        name="take_far",
        compiler_params=small(12),
    )(place, asked, *items)


def take_near(place, slots, asked, which_up, which_down, items, passing, axes, width):
    def kernel(place_ref, slot_ref, asked_ref, *refs):
        item_refs, (pass_up, pass_down), (to_up, to_down, own) = refs[:5], refs[5:7], refs[7:10]
        coords = coords_of(place_ref)
        for i in range(8):
            for which, through, out in ((which_up, pass_up, to_up), (which_down, pass_down, to_down)):
                slot = asked_ref[which, i]

                def store(value, out=out, i=i):
                    out[i] = value

                if (i < 4) == (out is to_up):
                    mine = field(slot, axes[2]) == coords[axes[2]]

                    @pl.when(mine)
                    def _(slot=slot, store=store):
                        copy_item(slot, coords, axes, item_refs, store)

                    @pl.when(jnp.logical_not(mine))
                    def _(through=through, store=store, i=i):
                        store(through[i % 4])

                else:
                    copy_item(slot, coords, axes, item_refs, store)

            def store_own(value, i=i):
                own[i] = value

            copy_item(slot_ref[i], coords, axes, item_refs, store_own)

    full = jax.ShapeDtypeStruct((8, RANK, width), jnp.bfloat16)
    return pl.pallas_call(
        kernel,
        out_shape=(full, full, full),
        in_specs=[smem_spec()] * 3 + [vmem_spec()] * 7,
        out_specs=(vmem_spec(),) * 3,
        name="take_near",
        compiler_params=small(16),
    )(place, slots, asked, *items, *passing)


def copy_arrived(i, slot, coords, axis, sources, store):
    rel = (field(slot, axis) - coords[axis]) & 3
    own, below, above = sources
    is_below = (rel != 0) & (rel != 1) if i < 4 else rel == 3
    is_above = rel == 1 if i < 4 else (rel != 0) & (rel != 3)
    for flag, ref in ((rel == 0, own), (is_below, below), (is_above, above)):

        @pl.when(flag)
        def _(ref=ref):
            store(ref)


def segments(index, length_ref):
    total = jnp.zeros_like(index)
    end = length_ref[0, 0]
    for p in range(8):
        total = total + (index >= end).astype(jnp.int32)
        if p < 7:
            end = end + length_ref[0, p + 1]
    return total


def pack(down, up, chosen, placement, splits, widths):
    firsts = [sum(splits[:p]) for p in range(3)]

    def kernel(chosen_ref, place_ref, down_hbm, up_hbm, *refs):
        parts, slot_ref, sems = refs[:3], refs[3], refs[4]
        copies = []

        def go(source, target):
            copies.append(pltpu.make_async_copy(source, target, sems.at[len(copies)]))
            copies[-1].start()

        go(down_hbm, parts[0].at[:, :, pl.ds(0, down.shape[2])])
        for p in range(3):
            wide = splits[p] * HEAD_DIM
            at = widths[p] - 3 * wide
            for j in range(3):
                go(up_hbm.at[:, j, :, pl.ds(firsts[p] * HEAD_DIM, wide)], parts[p].at[:, :, pl.ds(at + j * wide, wide)])
        lane = lax.broadcasted_iota(jnp.int32, (RANK, INFO), 1)
        note = jnp.zeros((RANK, INFO), jnp.int32)
        for i in range(8):
            slot = place_ref[chosen_ref[0, i]]
            slot_ref[i] = slot
            note = jnp.where(lane == i, slot, note)
        note = note.astype(jnp.float32).astype(jnp.bfloat16)
        for p in range(3):
            for k in range(4):
                parts[p][k, :, widths[p] :] = note
        for c in copies:
            c.wait()

    return pl.pallas_call(
        kernel,
        out_shape=tuple(jax.ShapeDtypeStruct((4, RANK, w + INFO), jnp.bfloat16) for w in widths)
        + (jax.ShapeDtypeStruct((8,), jnp.int32),),
        in_specs=[smem_spec(), smem_spec(), any_spec(), any_spec()],
        out_specs=(vmem_spec(),) * 3 + (smem_spec(),),
        scratch_shapes=[pltpu.SemaphoreType.DMA((10,))],
        name="pack",
        compiler_params=small(8),
    )(chosen, placement, down, up)


def read_asked(arrays, ats):
    count = len(arrays)

    def kernel(*refs):
        sources, out, buf, sems = refs[:count], refs[count], refs[count + 1], refs[count + 2]
        copies = [
            pltpu.make_async_copy(sources[n].at[0, :, pl.ds(ats[n], INFO)], buf.at[n], sems.at[n]) for n in range(count)
        ]
        for c in copies:
            c.start()
        for c in copies:
            c.wait()
        for n in range(count):
            out[n : n + 1, :] = buf[n].astype(jnp.float32)[0:1].astype(jnp.int32)

    return pl.pallas_call(
        kernel,
        out_shape=jax.ShapeDtypeStruct((count, INFO), jnp.int32),
        in_specs=[any_spec()] * count,
        out_specs=vmem_spec(),
        scratch_shapes=[pltpu.VMEM((count, RANK, INFO), jnp.bfloat16), pltpu.SemaphoreType.DMA((count,))],
        name="read_asked",
        compiler_params=small(2),
    )(*arrays)


def cut(below, above):
    count, rank, width = below.shape
    half = count // 2

    def kernel(below_ref, above_ref, lo, hi, sems):
        first = pltpu.make_async_copy(below_ref.at[pl.ds(0, half)], lo, sems.at[0])
        second = pltpu.make_async_copy(above_ref.at[pl.ds(half, half)], hi, sems.at[1])
        first.start()
        second.start()
        first.wait()
        second.wait()

    return pl.pallas_call(
        kernel,
        out_shape=(jax.ShapeDtypeStruct((half, rank, width), jnp.bfloat16),) * 2,
        in_specs=[any_spec()] * 2,
        out_specs=(vmem_spec(),) * 2,
        scratch_shapes=[pltpu.SemaphoreType.DMA((2,))],
        name="cut",
        compiler_params=small(4),
    )(below, above)


def rank_part(place, slots, lengths, normed, arrived, feat):
    tok = normed.shape[0]
    axis = AXES[0][2]

    def kernel(place_ref, slot_ref, length_ref, x_ref, own, below, above, out_ref, down):
        coords = coords_of(place_ref)
        for i in range(8):

            def store(ref, i=i):
                down[i * RANK : (i + 1) * RANK, :] = ref[i, :, 0:feat]

            copy_arrived(i, slot_ref[i], coords, axis, (own, below, above), store)
        mine = x_ref[:, pl.ds(pl.multiple_of(place_ref[3] * feat, feat), feat)]
        proj = lax.dot_general(mine, down[...], (((1,), (1,)), ((), ())), preferred_element_type=jnp.float32)
        rows = lax.broadcasted_iota(jnp.int32, proj.shape, 0)
        cols = lax.broadcasted_iota(jnp.int32, proj.shape, 1)
        out_ref[...] = jnp.where(segments(rows, length_ref) == (cols >> 4), proj, 0.0)

    return pl.pallas_call(
        kernel,
        out_shape=jax.ShapeDtypeStruct((tok, 8 * RANK), jnp.float32),
        in_specs=[smem_spec()] * 3 + [vmem_spec()] * 4,
        out_specs=vmem_spec(),
        scratch_shapes=[pltpu.VMEM((8 * RANK, feat), jnp.bfloat16)],
        name="rank_part",
        compiler_params=small(12),
    )(place, slots, lengths, normed, *arrived)


def project(normed, weight, which):
    tok, width = normed.shape
    cols = weight.shape[2]
    tile = 512

    def kernel(x_ref, w_ref, o_ref):
        o_ref[...] = jnp.dot(x_ref[...], w_ref[...], preferred_element_type=jnp.float32)

    return pl.pallas_call(
        kernel,
        out_shape=jax.ShapeDtypeStruct((tok, cols), jnp.float32),
        grid=(cols // tile,),
        in_specs=[
            pl.BlockSpec((tok, width), lambda n: (0, 0)),
            pl.BlockSpec((None, width, tile), lambda n: (which, 0, n)),
        ],
        out_specs=pl.BlockSpec((tok, tile), lambda n: (0, n)),
        name="project",
        compiler_params=small(20),
        cost_estimate=pl.CostEstimate(
            flops=2 * tok * width * cols, transcendentals=0, bytes_accessed=2 * width * cols + 2 * tok * width + 4 * tok * cols
        ),
    )(normed, weight)


def tail(place, slots, lengths, slopes, act, act_other, base, arrived, out_weight, heads, splits, widths):
    tok = act.shape[0]
    cols = base[0].shape[1]
    model = out_weight.shape[1]
    scale = 1.0 / math.sqrt(HEAD_DIM)
    half = tok // 2
    chunk = 4
    rows_w = cols // chunk
    up_widths = [3 * HEAD_DIM * n for n in splits]
    skips = [w - u for w, u in zip(widths, up_widths)]
    firsts = [sum(splits[:p]) for p in range(3)]

    def kernel(place_ref, slot_ref, length_ref, slope_ref, act_ref, other_ref, *refs):
        base_refs, arrived_refs, w_ref = refs[:3], refs[3:12], refs[12]
        keep_ref, send_ref = refs[13:15]
        ups, (att, base_buf, w_buf, base_sems, w_sems) = refs[15:18], refs[18:23]
        coords = coords_of(place_ref)

        def base_copy(p, j):
            lanes = pl.ds(firsts[p] * HEAD_DIM, splits[p] * HEAD_DIM)
            return pltpu.make_async_copy(base_refs[j].at[:, lanes], base_buf.at[j, :, lanes], base_sems.at[p, j])

        def w_copy(k):
            rows = pl.ds(k * rows_w, rows_w)
            return pltpu.make_async_copy(w_ref.at[rows], w_buf.at[rows], w_sems.at[k])

        for p in range(3):
            for j in range(3):
                base_copy(p, j).start()
        for k in range(chunk):
            w_copy(k).start()
        for p in range(3):
            for i in range(8):

                def store(ref, p=p, i=i):
                    ups[p][i * RANK : (i + 1) * RANK, :] = ref[i, :, skips[p] :]

                copy_arrived(i, slot_ref[i], coords, AXES[p][2], arrived_refs[3 * p : 3 * p + 3], store)
        rows = lax.broadcasted_iota(jnp.int32, (tok, 128), 0)
        starts = jnp.maximum((rows >> 6) * 64 - 64, 0)
        keys_at = lax.broadcasted_iota(jnp.int32, (tok, 128), 1) + starts
        allowed = (segments(rows, length_ref) == segments(keys_at, length_ref)) & (keys_at <= rows)
        apart = (keys_at - rows).astype(jnp.float32)
        low = (act_ref[...] + other_ref[...]).astype(jnp.bfloat16)
        core = place_ref[3]
        for p in range(3):
            for j in range(3):
                base_copy(p, j).wait()
            for t in range(splits[p]):
                h = firsts[p] + t
                mine = []
                for j in range(3):
                    at = (j * splits[p] + t) * HEAD_DIM
                    delta = jnp.dot(low, ups[p][:, at : at + HEAD_DIM], preferred_element_type=jnp.float32)
                    delta = delta.astype(jnp.bfloat16).astype(jnp.float32)
                    whole = base_buf[j, :, h * HEAD_DIM : (h + 1) * HEAD_DIM] + LOWRANK_SCALE * delta
                    mine.append(whole.astype(jnp.bfloat16))
                q, k, v = mine
                blocks = []
                for b in range(4):
                    w0 = max(64 * b - 64, 0)
                    blocks.append(
                        lax.dot_general(
                            q[64 * b : 64 * b + 64],
                            k[w0 : w0 + 128],
                            (((1,), (1,)), ((), ())),
                            preferred_element_type=jnp.float32,
                        )
                    )
                s = jnp.concatenate(blocks, 0)
                s = jnp.where(allowed, s * scale + slope_ref[h] * apart, -jnp.inf)
                e = jnp.exp(s - jnp.max(s, -1, keepdims=True))
                pr = (e / jnp.sum(e, -1, keepdims=True)).astype(jnp.bfloat16)
                outs = []
                for b in range(4):
                    w0 = max(64 * b - 64, 0)
                    outs.append(
                        jnp.dot(pr[64 * b : 64 * b + 64], v[w0 : w0 + 128], preferred_element_type=jnp.float32)
                    )
                o = jnp.concatenate(outs, 0).astype(jnp.bfloat16)
                lanes = slice(h * HEAD_DIM, (h + 1) * HEAD_DIM)
                for m in range(2):
                    at = pl.multiple_of(((core + m) & 1) * half, half)
                    att[pl.ds(at, half), lanes] = o[m * half : (m + 1) * half]
        for k in range(chunk):
            w_copy(k).wait()
        n_tile = 512
        for n in range(model // n_tile):
            lanes = slice(n * n_tile, (n + 1) * n_tile)
            part = jnp.dot(att[...], w_buf[:, lanes], preferred_element_type=jnp.float32).astype(jnp.bfloat16)
            keep_ref[:, lanes] = part[:half]
            send_ref[:, lanes] = part[half:]

    half_out = jax.ShapeDtypeStruct((half, model), jnp.bfloat16)
    return pl.pallas_call(
        kernel,
        out_shape=(half_out, half_out),
        in_specs=[smem_spec()] * 4 + [vmem_spec()] * 2 + [any_spec()] * 3 + [vmem_spec()] * 9 + [any_spec()],
        out_specs=(vmem_spec(),) * 2,
        scratch_shapes=[pltpu.VMEM((8 * RANK, w), jnp.bfloat16) for w in up_widths]
        + [
            pltpu.VMEM((tok, cols), jnp.bfloat16),
            pltpu.VMEM((3, tok, cols), jnp.float32),
            pltpu.VMEM((cols, model), jnp.bfloat16),
            pltpu.SemaphoreType.DMA((3, 3)),
            pltpu.SemaphoreType.DMA((chunk,)),
        ],
        name="tail",
        compiler_params=pltpu.CompilerParams(vmem_limit_bytes=44 * 1024 * 1024),
    )(place, slots, lengths, slopes, act, act_other, *base, *[a for part in arrived for a in part], out_weight)


def on_device(
    tokens,
    layer_norm_gain,
    query_key_value_weight,
    output_weight,
    stored_down_weight,
    stored_up_weight,
    group_prompt_length,
    prompt_adapter_index,
    placement,
):
    tok_count, width = tokens.shape
    tp_index = lax.axis_index("tp")
    req_index = lax.axis_index("req")
    head_part = query_key_value_weight.shape[2]
    local_heads = head_part // HEAD_DIM
    half = tok_count // 2

    place = jnp.stack([req_index & 3, (req_index >> 2) & 3, (req_index >> 4) & 3, tp_index]).astype(jnp.int32)

    down = jnp.transpose(stored_down_weight, (0, 2, 1))
    up = jnp.transpose(stored_up_weight, (0, 2, 1, 3))
    splits = (2, 7, 7)
    widths = [3 * HEAD_DIM * n + (head_part if p == 0 else 0) for p, n in enumerate(splits)]
    *own, slots = pack(down, up, prompt_adapter_index, placement, splits, widths)

    below1, above1, far1 = {}, {}, {}
    for p in range(3):
        axis = AXES[p][0]
        far1[p] = shift(own[p], axis, 2)
        below1[p] = shift(own[p], axis, 1)
        above1[p] = shift(own[p], axis, -1)

    asked = read_asked(
        [a for p in range(3) for a in (far1[p], above1[p], below1[p])], [widths[p] for p in range(3) for _ in range(3)]
    )

    wide = tokens.astype(jnp.float32)
    mean = jnp.mean(wide, -1, keepdims=True)
    centred = wide - mean
    variance = jnp.mean(centred * centred, -1, keepdims=True)
    normed = (centred * lax.rsqrt(variance + EPS) * layer_norm_gain.astype(jnp.float32)).astype(jnp.bfloat16)
    weight = jnp.transpose(query_key_value_weight, (1, 0, 2))
    base = [project(normed, weight, j) for j in range(3)]

    gathered = []
    for p in range(3):
        w = widths[p]
        gathered.append(jnp.concatenate([a[:, :, :w] for a in (own[p], above1[p], far1[p], below1[p])], 0))
    below2 = [shift(gathered[p], AXES[p][1], 1) for p in range(3)]
    above2 = [shift(gathered[p], AXES[p][1], -1) for p in range(3)]
    below2, above2, base = lax.optimization_barrier((below2, above2, base))
    halves = [cut(below2[p], above2[p]) for p in range(3)]
    far_lo = [shift(halves[p][0], AXES[p][1], 1) for p in range(3)]
    far_hi = [shift(halves[p][1], AXES[p][1], -1) for p in range(3)]

    arrived = []
    for p in range(3):
        axes = AXES[p]
        w = widths[p]
        items = (gathered[p], below2[p], above2[p], far_lo[p], far_hi[p])
        (giver,) = [g for g in range(3) if AXES[g][0] == axes[2]]
        t_up, t_down = take_far(place, asked, 3 * giver, items, axes, w)
        passing = (shift(t_up, axes[2], 1), shift(t_down, axes[2], -1))
        s_up, s_down, mine = take_near(
            place, slots, asked, 3 * giver + 1, 3 * giver + 2, items, passing, axes, w
        )
        arrived.append((mine, shift(s_up, axes[2], 1), shift(s_down, axes[2], -1)))

    swap = [(0, 1), (1, 0)]
    act = rank_part(place, slots, group_prompt_length, normed, arrived[0], head_part)
    act_other = lax.ppermute(act, "tp", swap)
    head_ids = tp_index * local_heads + jnp.arange(local_heads, dtype=jnp.int32)
    slopes = jnp.exp2(-8.0 * (head_ids.astype(jnp.float32) + 1.0) / HEADS)
    keep, send = tail(
        place, slots, group_prompt_length, slopes, act, act_other, base, arrived, output_weight, local_heads, splits, widths
    )
    got = lax.ppermute(send, "tp", swap)
    residual = lax.dynamic_slice_in_dim(tokens, tp_index * half, half, 0)
    return (keep.astype(jnp.float32) + got.astype(jnp.float32) + residual.astype(jnp.float32)).astype(jnp.bfloat16)


def solution(mesh):
    in_specs = (
        P("req", None),
        P(),
        P(None, None, "tp"),
        P("tp", None),
        P("req", "tp", None),
        P("req", None, None, "tp"),
        P("req", None),
        P("req", None),
        P(),
    )
    out_specs = P(("req", "tp"), None)
    return jax.shard_map(on_device, mesh=mesh, in_specs=in_specs, out_specs=out_specs, check_vma=False)
```
